32 devices in a mesh: dp: 4 (over y, core), expert: 8 (over z, x).
Axes of the slice: x: 2, y: 2, z: 4, core: 2. Of those that a mesh axis runs over, the one named last changes fastest.
Arguments:
- tokens: bfloat16 [8, 16, 4096], P('expert', None, 'dp'), may hold values from -6 to 6
- routes: int32 [8, 16, 8], P('expert'), may hold values from 0 to 7, all different within a row; in each aligned block of 16 rows (0 to 15, 16 to 31, ..., all dimensions but the last counted through in order) at most 16 rows name the same one
- gates: float32 [8, 16, 8], P('expert'), may hold values from 0.05 to 0.3
- plan: int32 [8], replicated, may hold values from 0 to 7, each once
- proj_weight: bfloat16 [8, 2, 4096, 768], P('expert', None, 'dp'), may hold values from -0.09375 to 0.09375
- proj_grad: bfloat16 [8, 2, 4096, 768], P('expert', None, 'dp'), may hold values from -6 to 6
- first_moment: float32 [8, 2, 4096, 768], P('expert', None, 'dp'), may hold values from -1.8 to 1.8
- second_moment: float32 [8, 2, 4096, 768], P('expert', None, 'dp'), may hold values from 0.01 to 0.1
- down_weight: bfloat16 [8, 768, 4096], P('expert', None, 'dp'), may hold values from -0.21875 to 0.21875
Outputs:
- out_tokens: bfloat16 [8, 16, 4096], P('expert', None, 'dp')
- new_proj: bfloat16 [8, 2, 4096, 768], P('expert', None, 'dp')
- new_down: bfloat16 [8, 768, 4096], P('expert', None, 'dp')
The draws below stay inside these ranges and needn't reach their ends.
Inputs may be any that keep to these rules, and one draw needn't show every extreme that they name: `routes`: each token names 8 different experts; within one group no expert is named by more than 16 tokens, and in some group some expert is named by exactly 16. Expert x moves to the owner plan[x]; every owner receives exactly one expert.
All inputs are finite; a program needn't handle non-finite values.
Results may differ from the reference program's by a relative error of at most 0.024.
Values may be sent and summed in bfloat16 or wider, within the bound.
A program may use at most 64 MiB of HBM per device.

```python
import math
import jax
import jax.numpy as jnp
import numpy as np
from jax import lax

D = 4096
F = 768
TOPK = 8
GROUP_TOK = 16
GROUPS = 8
EXPERTS = 8
MOST = 16
N_DP = 4


def shard_levels(rng, shape, pieces, low, largest):
    factor_of = 1.0
    for axis_at, parts in pieces:
        heights = jax.random.uniform(jax.random.fold_in(jax.random.fold_in(rng, 6), axis_at), (parts,), jnp.float32, low / len(pieces), largest / len(pieces))
        factor_of = factor_of * jnp.repeat(jnp.exp(heights), shape[axis_at] // parts).reshape((-1,) + (1,) * (len(shape) - 1 - axis_at))
    return factor_of


def shared_out(stream_key, own, number, rows, amount, top, reach, skew):
    order = jax.random.permutation(stream_key, amount)
    packed, usual = shares(amount, rows * top, reach, skew, True), shares(amount, rows * top, reach, skew, False)
    places = jnp.arange(amount)

    def named(tallies, offset_by):
        used = int((tallies > 0).sum())
        fixed = max(1, used // 4)
        moved = fixed + (places - fixed + offset_by * (used - fixed)) % max(1, amount - fixed)
        return jnp.zeros((amount,), jnp.int32).at[order[jnp.where(places < fixed, places, moved)]].set(jnp.asarray(tallies, jnp.int32))

    tallies = jnp.where(number % 4 == 0, named(packed, number // 4), named(usual, number - number // 4 - 1))
    mixed = jax.random.permutation(jax.random.fold_in(own, 3), amount)
    source_of, receiver = mixed[0:amount // 2 * 2:2], mixed[1:amount // 2 * 2:2]
    slack = jnp.minimum(tallies[source_of] - 1, reach - tallies[receiver]) // 2
    slack = jnp.where((source_of == order[0]) | (receiver == order[0]) | (tallies[receiver] == 0), 0, jnp.maximum(slack, 0))
    moved = jax.random.randint(jax.random.fold_in(own, 4), (amount // 2,), 0, 1 << 20) % (slack + 1)
    tallies = tallies.at[source_of].add(-moved).at[receiver].add(moved)
    labels = jnp.searchsorted(jnp.cumsum(tallies), jnp.arange(rows * top), side="right").astype(jnp.int32)
    listing = labels.reshape(top, rows).T
    listing = listing[jax.random.permutation(jax.random.fold_in(own, 1), rows)]
    offset_by = jax.random.randint(jax.random.fold_in(own, 2), (rows, 1), 0, top)
    return jnp.take_along_axis(listing, (jnp.arange(top)[None, :] + offset_by) % top, axis=1)


def shares(count, total, limit, skew, full):
    loads = [(1 << 20) // math.isqrt(standing ** skew) + 1 for standing in range(1, count + 1)]
    largest = limit if full else min(limit, max(-(-total // count), total * loads[0] // sum(loads)))
    least = 1 if total - largest >= count - 1 else 0
    counts, rest = [largest] + [least] * (count - 1), total - largest - least * (count - 1)
    while rest > 0:
        candidates = [i for i in range(1, count) if counts[i] < largest] or [i for i in range(1, count) if counts[i] < limit]
        mass, remaining = sum([loads[i] for i in candidates]), rest
        for i in candidates:
            more = min(limit - counts[i], max(1, remaining * loads[i] // mass), rest)
            counts[i] = counts[i] + more
            rest = rest - more
    return np.array(counts)


def centred(stream_key, shape, width, bound, split=(), held_as=jnp.bfloat16):
    loudness = shard_levels(stream_key, shape, split, -0.22, 0.18) if split else 1.0
    values = jax.random.normal(stream_key, shape, jnp.float32) * width * loudness
    return jnp.minimum(jnp.maximum(values, -bound), bound).astype(held_as)


def setup_inputs(seed: int = 0) -> dict:
    key_list = jax.random.split(jax.random.key(seed), 10)
    tokens = centred(key_list[0], (GROUPS, GROUP_TOK, D), 1.0, 6.0, ((0, 8), (2, 4)))
    routes_keys = jax.random.split(jax.random.fold_in(key_list[1], 1), GROUPS * GROUP_TOK // GROUP_TOK)
    routes_turns = jax.random.permutation(jax.random.fold_in(key_list[1], 3), GROUPS * GROUP_TOK // GROUP_TOK)
    routes = jax.vmap(lambda own, number: shared_out(jax.random.fold_in(key_list[1], 2), own, number, GROUP_TOK, EXPERTS, TOPK, MOST, 2))(routes_keys, routes_turns).reshape((GROUPS, GROUP_TOK, TOPK))
    gates = jnp.clip(0.05 + 0.25 * jax.random.uniform(key_list[2], (GROUPS, GROUP_TOK, TOPK), jnp.float32) ** shard_levels(key_list[2], (GROUPS, GROUP_TOK, TOPK), ((0, 8),), -0.2, 0.2), 0.05, 0.3)
    plan = jax.random.permutation(key_list[3], EXPERTS).astype(jnp.int32)
    proj_weight = centred(key_list[4], (EXPERTS, 2, D, F), D ** -0.5, 0.09375, ((0, 8), (2, 4)))
    proj_grad = centred(key_list[5], (EXPERTS, 2, D, F), 1.0, 6.0, ((0, 8), (2, 4)))
    first_moment = centred(key_list[6], (EXPERTS, 2, D, F), 0.3, 1.8, ((0, 8), (2, 4)), jnp.float32)
    second_moment = jnp.clip(jnp.exp(math.log(0.1) - 2.3025851 * jax.random.uniform(key_list[7], (EXPERTS, 2, D, F), jnp.float32) ** shard_levels(key_list[7], (EXPERTS, 2, D, F), ((0, 8), (2, 4)), -0.2, 0.2)), 0.01, 0.1)
    down_weight = centred(key_list[8], (EXPERTS, F, D), F ** -0.5, 0.21875, ((0, 8), (2, 4)))
    return dict(tokens=tokens, routes=routes, gates=gates, plan=plan, proj_weight=proj_weight, proj_grad=proj_grad, first_moment=first_moment, second_moment=second_moment, down_weight=down_weight)


learning_rate = 0.01
beta_first = 0.9
beta_second = 0.999
adam_epsilon = 1e-08
bias_first = 1.0 - 0.9 ** 10
bias_second = 1.0 - 0.999 ** 10

def adam_update(weights, grads, first_moment, second_moment):
    grad_float = grads.astype(jnp.float32)
    first_new = beta_first * first_moment + (1.0 - beta_first) * grad_float
    second_new = beta_second * second_moment + (1.0 - beta_second) * grad_float * grad_float
    adam_step = first_new / bias_first / (jnp.sqrt(second_new / bias_second) + adam_epsilon)
    return (weights.astype(jnp.float32) - learning_rate * adam_step).astype(jnp.bfloat16)

def reference(tokens, routes, gates, plan, proj_weight, proj_grad, first_moment, second_moment, down_weight):
    updated = adam_update(proj_weight, proj_grad, first_moment, second_moment)
    new_proj = jnp.zeros_like(updated).at[plan].set(updated)
    new_down = jnp.zeros_like(down_weight).at[plan].set(down_weight)
    slot_ids = jnp.arange(MOST, dtype=jnp.int32)
    token_float = tokens.astype(jnp.float32)
    block_width = D // N_DP

    def one_expert(running, expert):
        matches = routes == expert
        routed = lax.optimization_barrier(jnp.sum(matches.astype(jnp.int32), axis=2))
        weighting = lax.optimization_barrier(jnp.sum(jnp.where(matches, gates, 0.0), axis=2))
        ranks = jnp.cumsum(routed, axis=1) - routed
        select = jnp.logical_and(ranks[:, None, :] == slot_ids[None, :, None], routed[:, None, :] > 0).astype(jnp.float32)
        slots = jnp.einsum('gst,gtd->gsd', select, token_float).astype(jnp.bfloat16).reshape(GROUPS * MOST, D)
        projection = updated[expert]
        joined = jnp.concatenate([projection[0], projection[1]], axis=1)
        slot_blocks = slots.reshape(GROUPS * MOST, N_DP, block_width).astype(jnp.float32)
        weight_blocks = joined.reshape(N_DP, block_width, 2 * F).astype(jnp.float32)
        partial_sums = jnp.einsum('snd,ndf->nsf', slot_blocks, weight_blocks)
        rounded = lax.optimization_barrier(partial_sums.astype(jnp.bfloat16))
        summed = lax.optimization_barrier(jnp.sum(rounded.astype(jnp.float32), axis=0))
        gate_act = summed[:, :F]
        up_act = summed[:, F:]
        hidden = (jax.nn.silu(gate_act) * up_act).astype(jnp.bfloat16)
        expert_out = jnp.dot(hidden, down_weight[expert], preferred_element_type=jnp.float32).astype(jnp.bfloat16)
        outputs = expert_out.reshape(GROUPS, MOST, D).astype(jnp.float32)
        running = running + jnp.einsum('gst,gsd->gtd', select * weighting[:, None, :], outputs)
        return (running, None)
    start_total = jnp.zeros((GROUPS, GROUP_TOK, D), jnp.float32)
    final_total, ignored = lax.scan(one_expert, start_total, jnp.arange(EXPERTS, dtype=jnp.int32))
    return (final_total.astype(jnp.bfloat16), new_proj, new_down)
```

```python
import itertools

import jax
import jax.numpy as jnp
import numpy as np
from jax import lax
from jax.sharding import PartitionSpec as P

learning_rate = 0.01
beta_first = 0.9
beta_second = 0.999
adam_epsilon = 1e-08
bias_first = 1.0 - 0.9**10
bias_second = 1.0 - 0.999**10


def adam_update(weights, grads, first_moment, second_moment):
    grad_float = grads.astype(jnp.float32)
    first_new = beta_first * first_moment + (1.0 - beta_first) * grad_float
    second_new = beta_second * second_moment + (1.0 - beta_second) * grad_float * grad_float
    adam_step = first_new / bias_first / (jnp.sqrt(second_new / bias_second) + adam_epsilon)
    return (weights.astype(jnp.float32) - learning_rate * adam_step).astype(jnp.bfloat16)


max_levels = 1


def partial_products(slots, updated):
    joined = jnp.concatenate([updated[0], updated[1]], axis=1)
    return jnp.dot(slots, joined, preferred_element_type=jnp.float32).astype(jnp.bfloat16)


def finish_rows(partials, down_local):
    width = down_local.shape[0]
    parts = lax.axis_size("dp")
    blocks = lax.all_to_all(
        partials.reshape(1, parts, -1, partials.shape[1]),
        "dp",
        split_axis=1,
        concat_axis=1,
        tiled=True,
    )
    summed = jnp.sum(blocks[0].astype(jnp.float32), axis=0)
    hidden = (jax.nn.silu(summed[:, :width]) * summed[:, width:]).astype(jnp.bfloat16)
    result = jnp.dot(
        lax.all_gather(hidden, "dp", axis=0, tiled=True),
        down_local,
        preferred_element_type=jnp.float32,
    )
    return result.astype(jnp.bfloat16)


def owner_exchange(pieces):
    return lax.all_to_all(pieces, "expert", split_axis=1, concat_axis=1, tiled=True)


def two_phase_migration(plan, updated, down_local):
    owners = lax.axis_size("expert")
    local_rows, width = updated.shape[1:]
    expert_ids = jnp.arange(owners, dtype=jnp.int32)
    spread_down = owner_exchange(down_local.reshape(1, owners, width // owners, local_rows))
    spread_proj = owner_exchange(updated.reshape(2, owners, local_rows // owners, width))
    inverse = jnp.sum(
        jnp.where(plan[None, :] == expert_ids[:, None], expert_ids[None, :], 0), axis=1
    )
    moved_down = owner_exchange(jnp.take(spread_down, inverse, axis=1))
    moved_proj = owner_exchange(jnp.take(spread_proj, inverse, axis=1))
    return moved_proj.reshape(2, local_rows, width), moved_down.reshape(width, local_rows)


def colour_table(levels):
    bits = np.array(list(itertools.product((0, 1), repeat=levels)), np.int32)
    return np.stack([bits, 1 - bits], axis=2).reshape(len(bits), 2 * levels)


def worst_cut(perm):
    worst = 0
    for cut in range(1, len(perm)):
        up = sum(1 for z, to in enumerate(perm) if z < cut <= to)
        worst = max(worst, up)
    return worst


def route_choice(plan, levels):
    owners = 2 * levels
    perms = list(itertools.permutations(range(levels)))
    colours = colour_table(levels)
    ids = jnp.arange(owners, dtype=jnp.int32)
    arrives = plan[:, None] == ids[None, :]
    landed = jnp.sum(jnp.where(arrives[None], colours[:, :, None], 0), axis=1)
    pair_sum = landed.reshape(-1, levels, 2).sum(axis=2)
    bad = jnp.sum((pair_sum != 1).astype(jnp.int32), axis=1)
    scale = np.repeat(levels ** np.arange(levels, dtype=np.int32), 2)
    term = (plan // 2) * scale
    codes = np.array([sum(to * levels**z for z, to in enumerate(p)) for p in perms], np.int32)
    costs = np.array([worst_cut(p) for p in perms], np.int32)
    keys = [
        jnp.sum(jnp.where(colours == colour, term[None, :], 0), axis=1) for colour in (0, 1)
    ]
    hits = [key[:, None] == codes[None, :] for key in keys]
    cost = sum(jnp.sum(jnp.where(hit, costs[None, :], 0), axis=1) for hit in hits)
    count = len(colours)
    order = (bad * (4 * levels) + cost) * count + jnp.arange(count, dtype=jnp.int32)
    chosen = jnp.arange(count, dtype=jnp.int32) == jnp.min(order) % count
    numbers = np.arange(len(perms), dtype=np.int32)
    picks = [
        jnp.sum(jnp.where(chosen[:, None] & hit, numbers[None, :], 0)) for hit in hits
    ]
    source = jnp.sum(jnp.where(chosen[:, None], colours, 0), axis=0)
    landing = jnp.sum(jnp.where(chosen[:, None], landed, 0), axis=0)
    return source, landing, picks, perms


def body(
    tokens, routes, gates, plan, proj_weight, proj_grad, first_moment, second_moment, down_weight
):
    owners = lax.axis_size("expert")
    updated = adam_update(proj_weight, proj_grad, first_moment, second_moment)[0]
    local_rows = updated.shape[1]
    width = updated.shape[2]
    group_tokens = tokens.shape[1]
    route_count = routes.shape[2]
    capacity = min(group_tokens, 3 * group_tokens * route_count // (2 * owners))
    down_local = down_weight[0]
    expert_ids = jnp.arange(owners, dtype=jnp.int32)
    target_match = routes[0][:, :, None] == expert_ids[None, None, :]
    routed = jnp.sum(target_match.astype(jnp.int32), axis=1)
    weighting = jnp.sum(jnp.where(target_match, gates[0][:, :, None], 0.0), axis=1)
    ranks = jnp.cumsum(routed, axis=0) - routed
    slot_ids = jnp.arange(capacity, dtype=jnp.int32)
    select = jnp.logical_and(
        ranks.T[:, None, :] == slot_ids[None, :, None], routed.T[:, None, :] > 0
    )
    dispatch_buf = jnp.einsum(
        "ost,td->osd", select.astype(jnp.bfloat16), tokens[0], preferred_element_type=jnp.float32
    ).astype(jnp.bfloat16)
    arrived = owner_exchange(dispatch_buf[None])
    slots = arrived.reshape(owners * capacity, local_rows)

    def experts(partials):
        expert_out = finish_rows(partials, down_local)
        return owner_exchange(expert_out.reshape(1, owners, capacity, local_rows))

    levels = owners // 2
    if levels > max_levels:
        new_proj, new_down = two_phase_migration(plan, updated, down_local)
        returned = experts(partial_products(slots, updated))
    else:
        new_proj, new_down, returned = routed_migration(
            plan, levels, updated, down_local, slots, experts
        )
    combine = select.astype(jnp.float32) * weighting.T[:, None, :]
    mixed = jnp.einsum(
        "ost,osd->td", combine, returned[0].astype(jnp.float32), precision=lax.Precision.HIGHEST
    )
    return (mixed.astype(jnp.bfloat16)[None], new_proj[None], new_down[None])


def routed_migration(plan, levels, updated, down_local, slots, experts):
    source, landing, picks, perms = route_choice(plan, levels)
    me = lax.axis_index("expert")
    line = me % 2
    at_me = jnp.arange(2 * levels, dtype=jnp.int32) == me
    colour = jnp.sum(jnp.where(at_me, source, 0))
    landing_colour = jnp.sum(jnp.where(at_me, landing, 0))
    kept_half = line ^ colour
    final_half = line ^ landing_colour
    across = [(e, e ^ 1) for e in range(2 * levels)]
    local_rows, width = updated.shape[1:]
    piece = local_rows // 2

    def swap(value):
        return lax.ppermute(value, "expert", across)

    def parted(halves):
        keep = jnp.where(kept_half == 0, halves[0], halves[1])
        send = jnp.where(kept_half == 0, halves[1], halves[0])
        return keep, send

    def coloured(keep, other):
        first = jnp.where(colour == 0, keep, other)
        second = jnp.where(colour == 0, other, keep)
        return first, second

    down_halves = down_local.reshape(2, width // 2, local_rows)
    keep, send = parted(down_halves)
    down_first, down_second = coloured(keep, swap(send))
    proj_parts = [
        parted(updated[:, i * piece : (i + 1) * piece]) for i in range(2)
    ]
    partials = partial_products(slots, updated)

    def along(perm):
        pairs = [(2 * z + x, 2 * to + x) for z, to in enumerate(perm) for x in (0, 1)]
        return lambda value: lax.ppermute(value, "expert", pairs)

    def first_stage(perm):
        move = along(perm)

        def run(down_first, proj_parts, partials):
            moved_down = move(down_first)
            moved, waiting = [], []
            for keep, send in proj_parts:
                first, second = coloured(keep, swap(send))
                moved.append(move(first))
                waiting.append(second)
            return moved_down, moved, waiting, experts(partials)

        return run

    def second_stage(perm):
        move = along(perm)

        def run(items, moved):
            landed = []
            for first, waiting in zip(moved, items):
                second = move(waiting)
                keep = jnp.where(landing_colour == 0, first, second)
                send = jnp.where(landing_colour == 0, second, first)
                other = swap(send)
                landed.append(
                    (
                        jnp.where(final_half == 0, keep, other),
                        jnp.where(final_half == 0, other, keep),
                    )
                )
            return landed

        return run

    moved_down, moved, waiting, returned = lax.switch(
        picks[0], [first_stage(p) for p in perms], down_first, proj_parts, partials
    )
    landed = lax.switch(
        picks[1],
        [second_stage(p) for p in perms],
        [down_second] + waiting,
        [moved_down] + moved,
    )
    new_down = jnp.concatenate(landed[0], axis=0)
    new_proj = jnp.stack(
        [jnp.concatenate([pair[h] for pair in landed[1:]], axis=0) for h in (0, 1)]
    )
    return new_proj, new_down, returned


def solution(mesh):
    in_specs = (
        P("expert", None, "dp"),
        P("expert", None, None),
        P("expert", None, None),
        P(),
        P("expert", None, "dp", None),
        P("expert", None, "dp", None),
        P("expert", None, "dp", None),
        P("expert", None, "dp", None),
        P("expert", None, "dp"),
    )
    out_specs = (P("expert", None, "dp"), P("expert", None, "dp", None), P("expert", None, "dp"))
    return jax.shard_map(body, mesh=mesh, in_specs=in_specs, out_specs=out_specs, check_vma=False)
```

```python
import itertools

import jax
import jax.numpy as jnp
import numpy as np
from jax import lax
from jax.sharding import PartitionSpec as P

learning_rate = 0.01
beta_first = 0.9
beta_second = 0.999
adam_epsilon = 1e-08
bias_first = 1.0 - 0.9**10
bias_second = 1.0 - 0.999**10


def adam_update(weights, grads, first_moment, second_moment):
    grad_float = grads.astype(jnp.float32)
    first_new = beta_first * first_moment + (1.0 - beta_first) * grad_float
    second_new = beta_second * second_moment + (1.0 - beta_second) * grad_float * grad_float
    adam_step = first_new / bias_first / (jnp.sqrt(second_new / bias_second) + adam_epsilon)
    return (weights.astype(jnp.float32) - learning_rate * adam_step).astype(jnp.bfloat16)


max_levels = 4


def partial_products(slots, updated):
    joined = jnp.concatenate([updated[0], updated[1]], axis=1)
    return jnp.dot(slots, joined, preferred_element_type=jnp.float32).astype(jnp.bfloat16)


def finish_rows(partials, down_local):
    width = down_local.shape[0]
    parts = lax.axis_size("dp")
    blocks = lax.all_to_all(
        partials.reshape(1, parts, -1, partials.shape[1]),
        "dp",
        split_axis=1,
        concat_axis=1,
        tiled=True,
    )
    summed = jnp.sum(blocks[0].astype(jnp.float32), axis=0)
    hidden = (jax.nn.silu(summed[:, :width]) * summed[:, width:]).astype(jnp.bfloat16)
    result = jnp.dot(
        lax.all_gather(hidden, "dp", axis=0, tiled=True),
        down_local,
        preferred_element_type=jnp.float32,
    )
    return result.astype(jnp.bfloat16)


def owner_exchange(pieces):
    return lax.all_to_all(pieces, "expert", split_axis=1, concat_axis=1, tiled=True)


def two_phase_migration(plan, updated, down_local):
    owners = lax.axis_size("expert")
    local_rows, width = updated.shape[1:]
    expert_ids = jnp.arange(owners, dtype=jnp.int32)
    spread_down = owner_exchange(down_local.reshape(1, owners, width // owners, local_rows))
    spread_proj = owner_exchange(updated.reshape(2, owners, local_rows // owners, width))
    inverse = jnp.sum(
        jnp.where(plan[None, :] == expert_ids[:, None], expert_ids[None, :], 0), axis=1
    )
    moved_down = owner_exchange(jnp.take(spread_down, inverse, axis=1))
    moved_proj = owner_exchange(jnp.take(spread_proj, inverse, axis=1))
    return moved_proj.reshape(2, local_rows, width), moved_down.reshape(width, local_rows)


def colour_table(levels):
    bits = np.array(list(itertools.product((0, 1), repeat=levels)), np.int32)
    return np.stack([bits, 1 - bits], axis=2).reshape(len(bits), 2 * levels)


def worst_cut(perm):
    worst = 0
    for cut in range(1, len(perm)):
        up = sum(1 for z, to in enumerate(perm) if z < cut <= to)
        worst = max(worst, up)
    return worst


def route_choice(plan, levels):
    owners = 2 * levels
    perms = list(itertools.permutations(range(levels)))
    colours = colour_table(levels)
    ids = jnp.arange(owners, dtype=jnp.int32)
    arrives = plan[:, None] == ids[None, :]
    landed = jnp.sum(jnp.where(arrives[None], colours[:, :, None], 0), axis=1)
    pair_sum = landed.reshape(-1, levels, 2).sum(axis=2)
    bad = jnp.sum((pair_sum != 1).astype(jnp.int32), axis=1)
    scale = np.repeat(levels ** np.arange(levels, dtype=np.int32), 2)
    term = (plan // 2) * scale
    codes = np.array([sum(to * levels**z for z, to in enumerate(p)) for p in perms], np.int32)
    costs = np.array([worst_cut(p) for p in perms], np.int32)
    keys = [
        jnp.sum(jnp.where(colours == colour, term[None, :], 0), axis=1) for colour in (0, 1)
    ]
    hits = [key[:, None] == codes[None, :] for key in keys]
    cost = sum(jnp.sum(jnp.where(hit, costs[None, :], 0), axis=1) for hit in hits)
    count = len(colours)
    order = (bad * (4 * levels) + cost) * count + jnp.arange(count, dtype=jnp.int32)
    chosen = jnp.arange(count, dtype=jnp.int32) == jnp.min(order) % count
    numbers = np.arange(len(perms), dtype=np.int32)
    picks = [
        jnp.sum(jnp.where(chosen[:, None] & hit, numbers[None, :], 0)) for hit in hits
    ]
    source = jnp.sum(jnp.where(chosen[:, None], colours, 0), axis=0)
    landing = jnp.sum(jnp.where(chosen[:, None], landed, 0), axis=0)
    return source, landing, picks, perms


def body(
    tokens, routes, gates, plan, proj_weight, proj_grad, first_moment, second_moment, down_weight
):
    owners = lax.axis_size("expert")
    updated = adam_update(proj_weight, proj_grad, first_moment, second_moment)[0]
    local_rows = updated.shape[1]
    width = updated.shape[2]
    group_tokens = tokens.shape[1]
    route_count = routes.shape[2]
    capacity = min(group_tokens, 3 * group_tokens * route_count // (2 * owners))
    down_local = down_weight[0]
    expert_ids = jnp.arange(owners, dtype=jnp.int32)
    target_match = routes[0][:, :, None] == expert_ids[None, None, :]
    routed = jnp.sum(target_match.astype(jnp.int32), axis=1)
    weighting = jnp.sum(jnp.where(target_match, gates[0][:, :, None], 0.0), axis=1)
    ranks = jnp.cumsum(routed, axis=0) - routed
    slot_ids = jnp.arange(capacity, dtype=jnp.int32)
    select = jnp.logical_and(
        ranks.T[:, None, :] == slot_ids[None, :, None], routed.T[:, None, :] > 0
    )
    dispatch_buf = jnp.einsum(
        "ost,td->osd", select.astype(jnp.bfloat16), tokens[0], preferred_element_type=jnp.float32
    ).astype(jnp.bfloat16)
    arrived = owner_exchange(dispatch_buf[None])
    slots = arrived.reshape(owners * capacity, local_rows)

    def experts(partials):
        expert_out = finish_rows(partials, down_local)
        return owner_exchange(expert_out.reshape(1, owners, capacity, local_rows))

    levels = owners // 2
    if levels > max_levels:
        new_proj, new_down = two_phase_migration(plan, updated, down_local)
        returned = experts(partial_products(slots, updated))
    else:
        new_proj, new_down, returned = routed_migration(
            plan, levels, updated, down_local, slots, experts
        )
    combine = select.astype(jnp.float32) * weighting.T[:, None, :]
    mixed = jnp.einsum(
        "ost,osd->td", combine, returned[0].astype(jnp.float32), precision=lax.Precision.HIGHEST
    )
    return (mixed.astype(jnp.bfloat16)[None], new_proj[None], new_down[None])


def routed_migration(plan, levels, updated, down_local, slots, experts):
    source, landing, picks, perms = route_choice(plan, levels)
    me = lax.axis_index("expert")
    line = me % 2
    at_me = jnp.arange(2 * levels, dtype=jnp.int32) == me
    colour = jnp.sum(jnp.where(at_me, source, 0))
    landing_colour = jnp.sum(jnp.where(at_me, landing, 0))
    kept_half = line ^ colour
    final_half = line ^ landing_colour
    across = [(e, e ^ 1) for e in range(2 * levels)]
    local_rows, width = updated.shape[1:]
    piece = local_rows // 1

    def swap(value):
        return lax.ppermute(value, "expert", across)

    def parted(halves):
        keep = jnp.where(kept_half == 0, halves[0], halves[1])
        send = jnp.where(kept_half == 0, halves[1], halves[0])
        return keep, send

    def coloured(keep, other):
        first = jnp.where(colour == 0, keep, other)
        second = jnp.where(colour == 0, other, keep)
        return first, second

    down_halves = down_local.reshape(2, width // 2, local_rows)
    kept, sent = parted(down_halves)
    early = [coloured(kept, swap(sent))]
    proj_parts = [
        parted(updated[:, i * piece : (i + 1) * piece]) for i in range(1)
    ]
    outside = 1
    early += [coloured(keep, swap(send)) for keep, send in proj_parts[:outside]]
    late = proj_parts[outside:]
    returned = experts(partial_products(slots, updated))
    firsts = [first for first, second in early]
    seconds = [second for first, second in early]

    def along(perm):
        pairs = [(2 * z + x, 2 * to + x) for z, to in enumerate(perm) for x in (0, 1)]
        return lambda value: lax.ppermute(value, "expert", pairs)

    def first_stage(perm):
        move = along(perm)

        def run(firsts, late):
            moved = [move(first) for first in firsts]
            waiting = []
            for keep, send in late:
                first, second = coloured(keep, swap(send))
                moved.append(move(first))
                waiting.append(second)
            return moved, waiting

        return run

    def land(first, second):
        keep = jnp.where(landing_colour == 0, first, second)
        send = jnp.where(landing_colour == 0, second, first)
        return keep, swap(send)

    inside = 0

    def second_stage(perm):
        move = along(perm)

        def run(seconds, moved):
            arrived = [move(second) for second in seconds]
            landed = [land(moved[i], arrived[i]) for i in range(inside)]
            return landed, arrived[inside:]

        return run

    moved, waiting = lax.switch(picks[0], [first_stage(p) for p in perms], firsts, late)
    landed, arrived = lax.switch(
        picks[1], [second_stage(p) for p in perms], seconds + waiting, moved
    )
    landed = landed + [land(f, s) for f, s in zip(moved[inside:], arrived)]
    halves = [
        (jnp.where(final_half == 0, keep, other), jnp.where(final_half == 0, other, keep))
        for keep, other in landed
    ]
    new_down = jnp.concatenate(halves[0], axis=0)
    new_proj = jnp.stack(
        [jnp.concatenate([pair[h] for pair in halves[1:]], axis=0) for h in (0, 1)]
    )
    return new_proj, new_down, returned


def solution(mesh):
    in_specs = (
        P("expert", None, "dp"),
        P("expert", None, None),
        P("expert", None, None),
        P(),
        P("expert", None, "dp", None),
        P("expert", None, "dp", None),
        P("expert", None, "dp", None),
        P("expert", None, "dp", None),
        P("expert", None, "dp"),
    )
    out_specs = (P("expert", None, "dp"), P("expert", None, "dp", None), P("expert", None, "dp"))
    return jax.shard_map(body, mesh=mesh, in_specs=in_specs, out_specs=out_specs, check_vma=False)
```

```python
import itertools

import jax
import jax.numpy as jnp
import numpy as np
from jax import lax
from jax.sharding import PartitionSpec as P

learning_rate = 0.01
beta_first = 0.9
beta_second = 0.999
adam_epsilon = 1e-08
bias_first = 1.0 - 0.9**10
bias_second = 1.0 - 0.999**10


def adam_update(weights, grads, first_moment, second_moment):
    grad_float = grads.astype(jnp.float32)
    first_new = beta_first * first_moment + (1.0 - beta_first) * grad_float
    second_new = beta_second * second_moment + (1.0 - beta_second) * grad_float * grad_float
    adam_step = first_new / bias_first / (jnp.sqrt(second_new / bias_second) + adam_epsilon)
    return (weights.astype(jnp.float32) - learning_rate * adam_step).astype(jnp.bfloat16)


max_levels = 4


def partial_products(slots, updated):
    joined = jnp.concatenate([updated[0], updated[1]], axis=1)
    return jnp.dot(slots, joined, preferred_element_type=jnp.float32).astype(jnp.bfloat16)


def dp_blocks(partials):
    parts = lax.axis_size("dp")
    return lax.all_to_all(
        partials.reshape(1, parts, -1, partials.shape[1]),
        "dp",
        split_axis=1,
        concat_axis=1,
        tiled=True,
    )


def finish_rows(blocks, down_local):
    width = down_local.shape[0]
    summed = jnp.sum(blocks[0].astype(jnp.float32), axis=0)
    hidden = (jax.nn.silu(summed[:, :width]) * summed[:, width:]).astype(jnp.bfloat16)
    result = jnp.dot(
        lax.all_gather(hidden, "dp", axis=0, tiled=True),
        down_local,
        preferred_element_type=jnp.float32,
    )
    return result.astype(jnp.bfloat16)


def owner_exchange(pieces):
    return lax.all_to_all(pieces, "expert", split_axis=1, concat_axis=1, tiled=True)


def two_phase_migration(plan, updated, down_local):
    owners = lax.axis_size("expert")
    local_rows, width = updated.shape[1:]
    expert_ids = jnp.arange(owners, dtype=jnp.int32)
    spread_down = owner_exchange(down_local.reshape(1, owners, width // owners, local_rows))
    spread_proj = owner_exchange(updated.reshape(2, owners, local_rows // owners, width))
    inverse = jnp.sum(
        jnp.where(plan[None, :] == expert_ids[:, None], expert_ids[None, :], 0), axis=1
    )
    moved_down = owner_exchange(jnp.take(spread_down, inverse, axis=1))
    moved_proj = owner_exchange(jnp.take(spread_proj, inverse, axis=1))
    return moved_proj.reshape(2, local_rows, width), moved_down.reshape(width, local_rows)


def colour_table(levels):
    bits = np.array(list(itertools.product((0, 1), repeat=levels)), np.int32)
    return np.stack([bits, 1 - bits], axis=2).reshape(len(bits), 2 * levels)


def worst_cut(perm):
    worst = 0
    for cut in range(1, len(perm)):
        up = sum(1 for z, to in enumerate(perm) if z < cut <= to)
        worst = max(worst, up)
    return worst


def route_choice(plan, levels):
    owners = 2 * levels
    perms = list(itertools.permutations(range(levels)))
    colours = colour_table(levels)
    ids = jnp.arange(owners, dtype=jnp.int32)
    arrives = plan[:, None] == ids[None, :]
    landed = jnp.sum(jnp.where(arrives[None], colours[:, :, None], 0), axis=1)
    pair_sum = landed.reshape(-1, levels, 2).sum(axis=2)
    bad = jnp.sum((pair_sum != 1).astype(jnp.int32), axis=1)
    scale = np.repeat(levels ** np.arange(levels, dtype=np.int32), 2)
    term = (plan // 2) * scale
    codes = np.array([sum(to * levels**z for z, to in enumerate(p)) for p in perms], np.int32)
    costs = np.array([worst_cut(p) for p in perms], np.int32)
    keys = [
        jnp.sum(jnp.where(colours == colour, term[None, :], 0), axis=1) for colour in (0, 1)
    ]
    hits = [key[:, None] == codes[None, :] for key in keys]
    cost = sum(jnp.sum(jnp.where(hit, costs[None, :], 0), axis=1) for hit in hits)
    count = len(colours)
    order = (bad * (4 * levels) + cost) * count + jnp.arange(count, dtype=jnp.int32)
    chosen = jnp.arange(count, dtype=jnp.int32) == jnp.min(order) % count
    numbers = np.arange(len(perms), dtype=np.int32)
    picks = [
        jnp.sum(jnp.where(chosen[:, None] & hit, numbers[None, :], 0)) for hit in hits
    ]
    source = jnp.sum(jnp.where(chosen[:, None], colours, 0), axis=0)
    landing = jnp.sum(jnp.where(chosen[:, None], landed, 0), axis=0)
    return source, landing, picks, perms


def body(
    tokens, routes, gates, plan, proj_weight, proj_grad, first_moment, second_moment, down_weight
):
    owners = lax.axis_size("expert")
    updated = adam_update(proj_weight, proj_grad, first_moment, second_moment)[0]
    local_rows = updated.shape[1]
    width = updated.shape[2]
    group_tokens = tokens.shape[1]
    route_count = routes.shape[2]
    capacity = min(group_tokens, 3 * group_tokens * route_count // (2 * owners))
    down_local = down_weight[0]
    expert_ids = jnp.arange(owners, dtype=jnp.int32)
    target_match = routes[0][:, :, None] == expert_ids[None, None, :]
    routed = jnp.sum(target_match.astype(jnp.int32), axis=1)
    weighting = jnp.sum(jnp.where(target_match, gates[0][:, :, None], 0.0), axis=1)
    ranks = jnp.cumsum(routed, axis=0) - routed
    slot_ids = jnp.arange(capacity, dtype=jnp.int32)
    select = jnp.logical_and(
        ranks.T[:, None, :] == slot_ids[None, :, None], routed.T[:, None, :] > 0
    )
    dispatch_buf = jnp.einsum(
        "ost,td->osd", select.astype(jnp.bfloat16), tokens[0], preferred_element_type=jnp.float32
    ).astype(jnp.bfloat16)
    arrived = owner_exchange(dispatch_buf[None])
    slots = arrived.reshape(owners * capacity, local_rows)

    def experts(blocks):
        expert_out = finish_rows(blocks, down_local)
        return owner_exchange(expert_out.reshape(1, owners, capacity, local_rows))

    blocks = dp_blocks(partial_products(slots, updated))
    levels = owners // 2
    if levels <= max_levels and foldable(local_rows, width):
        new_proj, new_down, returned = routed_migration(
            plan, levels, updated, down_local, blocks, experts
        )
    else:
        new_proj, new_down = two_phase_migration(plan, updated, down_local)
        returned = experts(blocks)
    combine = select.astype(jnp.float32) * weighting.T[:, None, :]
    mixed = jnp.einsum(
        "ost,osd->td", combine, returned[0].astype(jnp.float32), precision=lax.Precision.HIGHEST
    )
    return (mixed.astype(jnp.bfloat16)[None], new_proj[None], new_down[None])


def foldable(local_rows, width):
    extra = local_rows - width
    return extra > 0 and width % extra == 0 and (width // 2) % (width // extra) == 0


def fold(half, width):
    strips = width // (half.shape[1] - width)
    tall = half.shape[0] // strips
    rest = [half[i * tall : (i + 1) * tall, width:] for i in range(strips)]
    return [half[:, :width], jnp.concatenate(rest, axis=1)]


def unfold(packed, rows, columns):
    width = packed.shape[1]
    extra = columns - width
    strips = [packed[rows:, i * extra : (i + 1) * extra] for i in range(width // extra)]
    return jnp.concatenate([packed[:rows], jnp.concatenate(strips, axis=0)], axis=1)


def routed_migration(plan, levels, updated, down_local, blocks, experts):
    source, landing, picks, perms = route_choice(plan, levels)
    me = lax.axis_index("expert")
    line = me % 2
    at_me = jnp.arange(2 * levels, dtype=jnp.int32) == me
    colour = jnp.sum(jnp.where(at_me, source, 0))
    landing_colour = jnp.sum(jnp.where(at_me, landing, 0))
    kept_half = line ^ colour
    final_half = line ^ landing_colour
    across = [(e, e ^ 1) for e in range(2 * levels)]
    local_rows, width = updated.shape[1:]
    half_width = width // 2
    folded = half_width * local_rows // width
    early = (local_rows - folded) // 2

    def swap(value):
        return lax.ppermute(value, "expert", across)

    def parted(first, second):
        keep = jnp.where(kept_half == 0, first, second)
        send = jnp.where(kept_half == 0, second, first)
        return keep, send

    def coloured(keep, other):
        first = jnp.where(colour == 0, keep, other)
        second = jnp.where(colour == 0, other, keep)
        return first, second

    packed = [
        jnp.concatenate(
            fold(down_local[h * half_width : (h + 1) * half_width], width)
            + [updated[h, :early]],
            axis=0,
        )
        for h in (0, 1)
    ]
    keep_p, send_p = parted(*packed)
    keep_q, send_q = parted(updated[0, early:], updated[1, early:])
    first_p, second_p = coloured(keep_p, swap(send_p))
    first_p, second_p, keep_q, send_q, blocks = lax.optimization_barrier(
        (first_p, second_p, keep_q, send_q, blocks)
    )

    def along(perm):
        pairs = [(2 * z + x, 2 * to + x) for z, to in enumerate(perm) for x in (0, 1)]
        return lambda value: lax.ppermute(value, "expert", pairs)

    def first_stage(perm):
        move = along(perm)
        return lambda value, crossing: (move(value), swap(crossing))

    def step(number, carry):
        first, second, crossing, keep, unused = carry
        moved, crossed = lax.switch(
            picks[0], [first_stage(p) for p in perms], first, crossing
        )
        arrived = lax.switch(picks[1], [along(p) for p in perms], second)
        is_last = number == 1
        next_first = jnp.where(is_last, moved, jnp.where(colour == 0, keep, crossed))
        next_second = jnp.where(is_last, arrived, jnp.where(colour == 0, crossed, keep))
        next_crossing = jnp.where(landing_colour == 0, arrived, moved)
        next_keep = jnp.where(is_last, keep, jnp.where(landing_colour == 0, moved, arrived))
        return next_first, next_second, next_crossing, next_keep, crossed

    moved, arrived, unused, own_p, other_p = lax.fori_loop(
        0, 2, step, (first_p, second_p, send_q, keep_q, keep_q)
    )
    moved, arrived, blocks = lax.optimization_barrier((moved, arrived, blocks))
    own_q = jnp.where(landing_colour == 0, moved, arrived)
    other_q = swap(jnp.where(landing_colour == 0, arrived, moved))
    returned = experts(blocks)
    halves_p = [jnp.where(final_half == h, own_p, other_p) for h in (0, 1)]
    halves_q = [jnp.where(final_half == h, own_q, other_q) for h in (0, 1)]
    new_down = jnp.concatenate(
        [unfold(half[:folded], half_width, local_rows) for half in halves_p], axis=0
    )
    new_proj = jnp.stack(
        [jnp.concatenate([p[folded:], q], axis=0) for p, q in zip(halves_p, halves_q)]
    )
    return new_proj, new_down, returned


def solution(mesh):
    in_specs = (
        P("expert", None, "dp"),
        P("expert", None, None),
        P("expert", None, None),
        P(),
        P("expert", None, "dp", None),
        P("expert", None, "dp", None),
        P("expert", None, "dp", None),
        P("expert", None, "dp", None),
        P("expert", None, "dp"),
    )
    out_specs = (P("expert", None, "dp"), P("expert", None, "dp", None), P("expert", None, "dp"))
    return jax.shard_map(body, mesh=mesh, in_specs=in_specs, out_specs=out_specs, check_vma=False)
```

```python
import itertools

import jax
import jax.numpy as jnp
import numpy as np
from jax import lax
from jax.sharding import PartitionSpec as P

learning_rate = 0.01
beta_first = 0.9
beta_second = 0.999
adam_epsilon = 1e-08
bias_first = 1.0 - 0.9**10
bias_second = 1.0 - 0.999**10


def adam_update(weights, grads, first_moment, second_moment):
    grad_float = grads.astype(jnp.float32)
    first_new = beta_first * first_moment + (1.0 - beta_first) * grad_float
    second_new = beta_second * second_moment + (1.0 - beta_second) * grad_float * grad_float
    adam_step = first_new / bias_first / (jnp.sqrt(second_new / bias_second) + adam_epsilon)
    return (weights.astype(jnp.float32) - learning_rate * adam_step).astype(jnp.bfloat16)


max_levels = 4


def partial_products(slots, pieces):
    total, start = 0.0, 0
    for updated in pieces:
        rows = updated.shape[1]
        joined = jnp.concatenate([updated[0], updated[1]], axis=1)
        total += jnp.dot(
            slots[:, start : start + rows], joined, preferred_element_type=jnp.float32
        )
        start += rows
    return total.astype(jnp.bfloat16)


def dp_blocks(partials):
    parts = lax.axis_size("dp")
    return lax.all_to_all(
        partials.reshape(1, parts, -1, partials.shape[1]),
        "dp",
        split_axis=1,
        concat_axis=1,
        tiled=True,
    )


def finish_rows(blocks, down_local):
    width = down_local.shape[0]
    summed = jnp.sum(blocks[0].astype(jnp.float32), axis=0)
    hidden = (jax.nn.silu(summed[:, :width]) * summed[:, width:]).astype(jnp.bfloat16)
    result = jnp.dot(
        lax.all_gather(hidden, "dp", axis=0, tiled=True),
        down_local,
        preferred_element_type=jnp.float32,
    )
    return result.astype(jnp.bfloat16)


def owner_exchange(pieces):
    return lax.all_to_all(pieces, "expert", split_axis=1, concat_axis=1, tiled=True)


def two_phase_migration(plan, updated, down_local):
    owners = lax.axis_size("expert")
    local_rows, width = updated.shape[1:]
    expert_ids = jnp.arange(owners, dtype=jnp.int32)
    spread_down = owner_exchange(down_local.reshape(1, owners, width // owners, local_rows))
    spread_proj = owner_exchange(updated.reshape(2, owners, local_rows // owners, width))
    inverse = jnp.sum(
        jnp.where(plan[None, :] == expert_ids[:, None], expert_ids[None, :], 0), axis=1
    )
    moved_down = owner_exchange(jnp.take(spread_down, inverse, axis=1))
    moved_proj = owner_exchange(jnp.take(spread_proj, inverse, axis=1))
    return moved_proj.reshape(2, local_rows, width), moved_down.reshape(width, local_rows)


def colour_table(levels):
    bits = np.array(list(itertools.product((0, 1), repeat=levels)), np.int32)
    return np.stack([bits, 1 - bits], axis=2).reshape(len(bits), 2 * levels)


def worst_cut(perm):
    worst = 0
    for cut in range(1, len(perm)):
        up = sum(1 for z, to in enumerate(perm) if z < cut <= to)
        worst = max(worst, up)
    return worst


def route_choice(plan, levels):
    owners = 2 * levels
    perms = list(itertools.permutations(range(levels)))
    colours = colour_table(levels)
    ids = jnp.arange(owners, dtype=jnp.int32)
    arrives = plan[:, None] == ids[None, :]
    landed = jnp.sum(jnp.where(arrives[None], colours[:, :, None], 0), axis=1)
    pair_sum = landed.reshape(-1, levels, 2).sum(axis=2)
    bad = jnp.sum((pair_sum != 1).astype(jnp.int32), axis=1)
    scale = np.repeat(levels ** np.arange(levels, dtype=np.int32), 2)
    term = (plan // 2) * scale
    codes = np.array([sum(to * levels**z for z, to in enumerate(p)) for p in perms], np.int32)
    costs = np.array([worst_cut(p) for p in perms], np.int32)
    keys = [
        jnp.sum(jnp.where(colours == colour, term[None, :], 0), axis=1) for colour in (0, 1)
    ]
    hits = [key[:, None] == codes[None, :] for key in keys]
    cost = sum(jnp.sum(jnp.where(hit, costs[None, :], 0), axis=1) for hit in hits)
    count = len(colours)
    order = (bad * (4 * levels) + cost) * count + jnp.arange(count, dtype=jnp.int32)
    chosen = jnp.arange(count, dtype=jnp.int32) == jnp.min(order) % count
    numbers = np.arange(len(perms), dtype=np.int32)
    picks = [
        jnp.sum(jnp.where(chosen[:, None] & hit, numbers[None, :], 0)) for hit in hits
    ]
    source = jnp.sum(jnp.where(chosen[:, None], colours, 0), axis=0)
    landing = jnp.sum(jnp.where(chosen[:, None], landed, 0), axis=0)
    return source, landing, picks, perms


def body(
    tokens, routes, gates, plan, proj_weight, proj_grad, first_moment, second_moment, down_weight
):
    owners = lax.axis_size("expert")
    local_rows = proj_weight.shape[2]
    width = proj_weight.shape[3]
    levels = owners // 2
    routable = levels <= max_levels and foldable(local_rows, width)
    cuts = [0, early_rows(local_rows, width), local_rows] if routable else [0, local_rows]
    pieces = [
        adam_update(
            proj_weight[0, :, a:b], proj_grad[0, :, a:b], first_moment[0, :, a:b], second_moment[0, :, a:b]
        )
        for a, b in zip(cuts[:-1], cuts[1:])
    ]
    group_tokens = tokens.shape[1]
    route_count = routes.shape[2]
    capacity = min(group_tokens, 3 * group_tokens * route_count // (2 * owners))
    down_local = down_weight[0]
    expert_ids = jnp.arange(owners, dtype=jnp.int32)
    target_match = routes[0][:, :, None] == expert_ids[None, None, :]
    routed = jnp.sum(target_match.astype(jnp.int32), axis=1)
    weighting = jnp.sum(jnp.where(target_match, gates[0][:, :, None], 0.0), axis=1)
    ranks = jnp.cumsum(routed, axis=0) - routed
    slot_ids = jnp.arange(capacity, dtype=jnp.int32)
    select = jnp.logical_and(
        ranks.T[:, None, :] == slot_ids[None, :, None], routed.T[:, None, :] > 0
    )
    dispatch_buf = jnp.einsum(
        "ost,td->osd", select.astype(jnp.bfloat16), tokens[0], preferred_element_type=jnp.float32
    ).astype(jnp.bfloat16)
    arrived = owner_exchange(dispatch_buf[None])
    slots = arrived.reshape(owners * capacity, local_rows)

    expert_out = finish_rows(dp_blocks(partial_products(slots, pieces)), down_local)
    expert_out = expert_out.reshape(1, owners, capacity, local_rows)
    if routable:
        new_proj, new_down, returned = routed_migration(
            plan, levels, pieces, down_local, arrived, expert_out
        )
    else:
        new_proj, new_down = two_phase_migration(plan, pieces[0], down_local)
        returned = owner_exchange(expert_out)
    combine = select.astype(jnp.float32) * weighting.T[:, None, :]
    mixed = jnp.einsum(
        "ost,osd->td", combine, returned[0].astype(jnp.float32), precision=lax.Precision.HIGHEST
    )
    return (mixed.astype(jnp.bfloat16)[None], new_proj[None], new_down[None])


def foldable(local_rows, width):
    extra = local_rows - width
    return extra > 0 and width % extra == 0 and (width // 2) % (width // extra) == 0


def early_rows(local_rows, width):
    return (local_rows - (width // 2) * local_rows // width) // 2


def fold(half, width):
    strips = width // (half.shape[1] - width)
    tall = half.shape[0] // strips
    rest = [half[i * tall : (i + 1) * tall, width:] for i in range(strips)]
    return [half[:, :width], jnp.concatenate(rest, axis=1)]


def unfold(packed, rows, columns):
    width = packed.shape[1]
    extra = columns - width
    strips = [packed[rows:, i * extra : (i + 1) * extra] for i in range(width // extra)]
    return jnp.concatenate([packed[:rows], jnp.concatenate(strips, axis=0)], axis=1)


def routed_migration(plan, levels, pieces, down_local, arrived, expert_out):
    source, landing, picks, perms = route_choice(plan, levels)
    me = lax.axis_index("expert")
    line = me % 2
    at_me = jnp.arange(2 * levels, dtype=jnp.int32) == me
    colour = jnp.sum(jnp.where(at_me, source, 0))
    landing_colour = jnp.sum(jnp.where(at_me, landing, 0))
    kept_half = line ^ colour
    final_half = line ^ landing_colour
    across = [(e, e ^ 1) for e in range(2 * levels)]
    local_rows, width = down_local.shape[1], pieces[0].shape[2]
    half_width = width // 2
    folded = half_width * local_rows // width
    updated_early, updated_late = pieces

    def swap(value):
        return lax.ppermute(value, "expert", across)

    def parted(first, second):
        keep = jnp.where(kept_half == 0, first, second)
        send = jnp.where(kept_half == 0, second, first)
        return keep, send

    def coloured(keep, other):
        first = jnp.where(colour == 0, keep, other)
        second = jnp.where(colour == 0, other, keep)
        return first, second

    packed = [
        jnp.concatenate(
            fold(down_local[h * half_width : (h + 1) * half_width], width)
            + [updated_early[h]],
            axis=0,
        )
        for h in (0, 1)
    ]
    keep_p, send_p = parted(*packed)
    keep_q, send_q = parted(updated_late[0], updated_late[1])
    send_p, ahead = lax.optimization_barrier((send_p, arrived))
    first_p, second_p = coloured(keep_p, swap(send_p))
    first_p, second_p, keep_q, send_q, expert_out = lax.optimization_barrier(
        (first_p, second_p, keep_q, send_q, expert_out)
    )

    def along(perm):
        pairs = [(2 * z + x, 2 * to + x) for z, to in enumerate(perm) for x in (0, 1)]
        return lambda value: lax.ppermute(value, "expert", pairs)

    def first_stage(perm):
        move = along(perm)
        return lambda value, crossing: (move(value), swap(crossing))

    def step(number, carry):
        first, second, crossing, keep, unused = carry
        moved, crossed = lax.switch(
            picks[0], [first_stage(p) for p in perms], first, crossing
        )
        arrived = lax.switch(picks[1], [along(p) for p in perms], second)
        is_last = number == 1
        next_first = jnp.where(is_last, moved, jnp.where(colour == 0, keep, crossed))
        next_second = jnp.where(is_last, arrived, jnp.where(colour == 0, crossed, keep))
        next_crossing = jnp.where(landing_colour == 0, arrived, moved)
        next_keep = jnp.where(is_last, keep, jnp.where(landing_colour == 0, moved, arrived))
        return next_first, next_second, next_crossing, next_keep, crossed

    moved, arrived, unused, own_p, other_p = lax.fori_loop(
        0, 2, step, (first_p, second_p, send_q, keep_q, keep_q)
    )
    moved, arrived, expert_out = lax.optimization_barrier((moved, arrived, expert_out))
    returned = owner_exchange(expert_out)
    own_q = jnp.where(landing_colour == 0, moved, arrived)
    send_q = jnp.where(landing_colour == 0, arrived, moved)
    send_q, returned = lax.optimization_barrier((send_q, returned))
    other_q = swap(send_q)
    halves_p = [jnp.where(final_half == h, own_p, other_p) for h in (0, 1)]
    halves_q = [jnp.where(final_half == h, own_q, other_q) for h in (0, 1)]
    new_down = jnp.concatenate(
        [unfold(half[:folded], half_width, local_rows) for half in halves_p], axis=0
    )
    new_proj = jnp.stack(
        [jnp.concatenate([p[folded:], q], axis=0) for p, q in zip(halves_p, halves_q)]
    )
    return new_proj, new_down, returned


def solution(mesh):
    in_specs = (
        P("expert", None, "dp"),
        P("expert", None, None),
        P("expert", None, None),
        P(),
        P("expert", None, "dp", None),
        P("expert", None, "dp", None),
        P("expert", None, "dp", None),
        P("expert", None, "dp", None),
        P("expert", None, "dp"),
    )
    out_specs = (P("expert", None, "dp"), P("expert", None, "dp", None), P("expert", None, "dp"))
    return jax.shard_map(body, mesh=mesh, in_specs=in_specs, out_specs=out_specs, check_vma=False)
```

```python
import itertools

import jax
import jax.numpy as jnp
import numpy as np
from jax import lax
from jax.sharding import PartitionSpec as P

learning_rate = 0.01
beta_first = 0.9
beta_second = 0.999
adam_epsilon = 1e-08
bias_first = 1.0 - 0.9**10
bias_second = 1.0 - 0.999**10


def adam_update(weights, grads, first_moment, second_moment):
    grad_float = grads.astype(jnp.float32)
    first_new = beta_first * first_moment + (1.0 - beta_first) * grad_float
    second_new = beta_second * second_moment + (1.0 - beta_second) * grad_float * grad_float
    adam_step = first_new / bias_first / (jnp.sqrt(second_new / bias_second) + adam_epsilon)
    return (weights.astype(jnp.float32) - learning_rate * adam_step).astype(jnp.bfloat16)


max_levels = 4


def partial_products(slots, pieces):
    total, start = 0.0, 0
    for updated in pieces:
        rows = updated.shape[1]
        joined = jnp.concatenate([updated[0], updated[1]], axis=1)
        total += jnp.dot(
            slots[:, start : start + rows], joined, preferred_element_type=jnp.float32
        )
        start += rows
    return total.astype(jnp.bfloat16)


def dp_blocks(partials):
    parts = lax.axis_size("dp")
    return lax.all_to_all(
        partials.reshape(1, parts, -1, partials.shape[1]),
        "dp",
        split_axis=1,
        concat_axis=1,
        tiled=True,
    )


def finish_rows(blocks, down_local):
    width = down_local.shape[0]
    summed = jnp.sum(blocks[0].astype(jnp.float32), axis=0)
    hidden = (jax.nn.silu(summed[:, :width]) * summed[:, width:]).astype(jnp.bfloat16)
    result = jnp.dot(
        lax.all_gather(hidden, "dp", axis=0, tiled=True),
        down_local,
        preferred_element_type=jnp.float32,
    )
    return result.astype(jnp.bfloat16)


def owner_exchange(pieces):
    return lax.all_to_all(pieces, "expert", split_axis=1, concat_axis=1, tiled=True)


def two_phase_migration(plan, updated, down_local):
    owners = lax.axis_size("expert")
    local_rows, width = updated.shape[1:]
    expert_ids = jnp.arange(owners, dtype=jnp.int32)
    spread_down = owner_exchange(down_local.reshape(1, owners, width // owners, local_rows))
    spread_proj = owner_exchange(updated.reshape(2, owners, local_rows // owners, width))
    inverse = jnp.sum(
        jnp.where(plan[None, :] == expert_ids[:, None], expert_ids[None, :], 0), axis=1
    )
    moved_down = owner_exchange(jnp.take(spread_down, inverse, axis=1))
    moved_proj = owner_exchange(jnp.take(spread_proj, inverse, axis=1))
    return moved_proj.reshape(2, local_rows, width), moved_down.reshape(width, local_rows)


def colour_table(levels):
    bits = np.array(list(itertools.product((0, 1), repeat=levels)), np.int32)
    return np.stack([bits, 1 - bits], axis=2).reshape(len(bits), 2 * levels)


def worst_cut(perm):
    worst = 0
    for cut in range(1, len(perm)):
        up = sum(1 for z, to in enumerate(perm) if z < cut <= to)
        worst = max(worst, up)
    return worst


def route_choice(plan, levels):
    owners = 2 * levels
    perms = list(itertools.permutations(range(levels)))
    colours = colour_table(levels)
    ids = jnp.arange(owners, dtype=jnp.int32)
    arrives = plan[:, None] == ids[None, :]
    landed = jnp.sum(jnp.where(arrives[None], colours[:, :, None], 0), axis=1)
    pair_sum = landed.reshape(-1, levels, 2).sum(axis=2)
    bad = jnp.sum((pair_sum != 1).astype(jnp.int32), axis=1)
    scale = np.repeat(levels ** np.arange(levels, dtype=np.int32), 2)
    term = (plan // 2) * scale
    codes = np.array([sum(to * levels**z for z, to in enumerate(p)) for p in perms], np.int32)
    costs = np.array([worst_cut(p) for p in perms], np.int32)
    keys = [
        jnp.sum(jnp.where(colours == colour, term[None, :], 0), axis=1) for colour in (0, 1)
    ]
    hits = [key[:, None] == codes[None, :] for key in keys]
    cost = sum(jnp.sum(jnp.where(hit, costs[None, :], 0), axis=1) for hit in hits)
    count = len(colours)
    order = (bad * (4 * levels) + cost) * count + jnp.arange(count, dtype=jnp.int32)
    chosen = jnp.arange(count, dtype=jnp.int32) == jnp.min(order) % count
    numbers = np.arange(len(perms), dtype=np.int32)
    picks = [
        jnp.sum(jnp.where(chosen[:, None] & hit, numbers[None, :], 0)) for hit in hits
    ]
    source = jnp.sum(jnp.where(chosen[:, None], colours, 0), axis=0)
    landing = jnp.sum(jnp.where(chosen[:, None], landed, 0), axis=0)
    return source, landing, picks, perms


def body(
    tokens, routes, gates, plan, proj_weight, proj_grad, first_moment, second_moment, down_weight
):
    owners = lax.axis_size("expert")
    local_rows = proj_weight.shape[2]
    width = proj_weight.shape[3]
    levels = owners // 2
    routable = levels <= max_levels and foldable(local_rows, width)

    def updated_rows(grads, a, b):
        return adam_update(
            proj_weight[0, :, a:b], grads[0, :, a:b], first_moment[0, :, a:b], second_moment[0, :, a:b]
        )

    group_tokens = tokens.shape[1]
    route_count = routes.shape[2]
    capacity = min(group_tokens, 3 * group_tokens * route_count // (2 * owners))
    down_local = down_weight[0]
    expert_ids = jnp.arange(owners, dtype=jnp.int32)
    target_match = routes[0][:, :, None] == expert_ids[None, None, :]
    routed = jnp.sum(target_match.astype(jnp.int32), axis=1)
    weighting = jnp.sum(jnp.where(target_match, gates[0][:, :, None], 0.0), axis=1)
    ranks = jnp.cumsum(routed, axis=0) - routed
    slot_ids = jnp.arange(capacity, dtype=jnp.int32)
    select = jnp.logical_and(
        ranks.T[:, None, :] == slot_ids[None, :, None], routed.T[:, None, :] > 0
    )
    dispatch_buf = jnp.einsum(
        "ost,td->osd", select.astype(jnp.bfloat16), tokens[0], preferred_element_type=jnp.float32
    ).astype(jnp.bfloat16)
    arrived = owner_exchange(dispatch_buf[None])
    slots = arrived.reshape(owners * capacity, local_rows)


    def experts(pieces):
        expert_out = finish_rows(dp_blocks(partial_products(slots, pieces)), down_local)
        return expert_out.reshape(1, owners, capacity, local_rows)

    if routable:
        early = early_rows(local_rows, width)
        new_proj, new_down, returned = routed_migration(
            plan,
            levels,
            updated_rows(proj_grad, 0, early),
            lambda grads: updated_rows(grads, early, local_rows),
            proj_grad,
            down_local,
            arrived,
            experts,
        )
    else:
        updated = updated_rows(proj_grad, 0, local_rows)
        new_proj, new_down = two_phase_migration(plan, updated, down_local)
        returned = owner_exchange(experts([updated]))
    combine = select.astype(jnp.float32) * weighting.T[:, None, :]
    mixed = jnp.einsum(
        "ost,osd->td", combine, returned[0].astype(jnp.float32), precision=lax.Precision.HIGHEST
    )
    return (mixed.astype(jnp.bfloat16)[None], new_proj[None], new_down[None])


def foldable(local_rows, width):
    extra = local_rows - width
    return extra > 0 and width % extra == 0 and (width // 2) % (width // extra) == 0


def early_rows(local_rows, width):
    return (local_rows - (width // 2) * local_rows // width) // 2


def fold(half, width):
    strips = width // (half.shape[1] - width)
    tall = half.shape[0] // strips
    rest = [half[i * tall : (i + 1) * tall, width:] for i in range(strips)]
    return [half[:, :width], jnp.concatenate(rest, axis=1)]


def unfold(packed, rows, columns):
    width = packed.shape[1]
    extra = columns - width
    strips = [packed[rows:, i * extra : (i + 1) * extra] for i in range(width // extra)]
    return jnp.concatenate([packed[:rows], jnp.concatenate(strips, axis=0)], axis=1)


def routed_migration(
    plan, levels, updated_early, late_rows, grads, down_local, arrived, experts
):
    source, landing, picks, perms = route_choice(plan, levels)
    me = lax.axis_index("expert")
    line = me % 2
    at_me = jnp.arange(2 * levels, dtype=jnp.int32) == me
    colour = jnp.sum(jnp.where(at_me, source, 0))
    landing_colour = jnp.sum(jnp.where(at_me, landing, 0))
    kept_half = line ^ colour
    final_half = line ^ landing_colour
    across = [(e, e ^ 1) for e in range(2 * levels)]
    local_rows, width = down_local.shape[1], updated_early.shape[2]
    half_width = width // 2
    folded = half_width * local_rows // width

    def swap(value):
        return lax.ppermute(value, "expert", across)

    def parted(first, second):
        keep = jnp.where(kept_half == 0, first, second)
        send = jnp.where(kept_half == 0, second, first)
        return keep, send

    def coloured(keep, other):
        first = jnp.where(colour == 0, keep, other)
        second = jnp.where(colour == 0, other, keep)
        return first, second

    packed = [
        jnp.concatenate(
            fold(down_local[h * half_width : (h + 1) * half_width], width)
            + [updated_early[h]],
            axis=0,
        )
        for h in (0, 1)
    ]
    keep_p, send_p = parted(*packed)
    send_p, grads, ahead = lax.optimization_barrier((send_p, grads, arrived))
    crossed_p = swap(send_p)
    updated_late = late_rows(grads)
    keep_q, send_q = parted(updated_late[0], updated_late[1])
    expert_out = experts([updated_early, updated_late])
    keep_p, crossed_p, keep_q, send_q, expert_out = lax.optimization_barrier(
        (keep_p, crossed_p, keep_q, send_q, expert_out)
    )

    def along(perm):
        pairs = [(2 * z + x, 2 * to + x) for z, to in enumerate(perm) for x in (0, 1)]
        return lambda value: lax.ppermute(value, "expert", pairs)

    def first_stage(perm):
        move = along(perm)
        return lambda value, crossing: (move(value), swap(crossing))

    def step(number, carry):
        keep, crossed, moved, arrived, unused = carry
        first, second = coloured(keep, crossed)
        own = jnp.where(landing_colour == 0, moved, arrived)
        other = jnp.where(landing_colour == 0, arrived, moved)
        crossing = jnp.where(number == 0, moved, other)
        moved, crossed = lax.switch(
            picks[0], [first_stage(p) for p in perms], first, crossing
        )
        arrived = lax.switch(picks[1], [along(p) for p in perms], second)
        return keep_q, crossed, moved, arrived, own

    unused, other_p, moved, arrived, own_p = lax.fori_loop(
        0, 2, step, (keep_p, crossed_p, send_q, send_q, send_q)
    )
    moved, arrived, expert_out = lax.optimization_barrier((moved, arrived, expert_out))
    returned = owner_exchange(expert_out)
    own_q = jnp.where(landing_colour == 0, moved, arrived)
    send_q = jnp.where(landing_colour == 0, arrived, moved)
    send_q, returned = lax.optimization_barrier((send_q, returned))
    other_q = swap(send_q)
    halves_p = [jnp.where(final_half == h, own_p, other_p) for h in (0, 1)]
    halves_q = [jnp.where(final_half == h, own_q, other_q) for h in (0, 1)]
    new_down = jnp.concatenate(
        [unfold(half[:folded], half_width, local_rows) for half in halves_p], axis=0
    )
    new_proj = jnp.stack(
        [jnp.concatenate([p[folded:], q], axis=0) for p, q in zip(halves_p, halves_q)]
    )
    return new_proj, new_down, returned


def solution(mesh):
    in_specs = (
        P("expert", None, "dp"),
        P("expert", None, None),
        P("expert", None, None),
        P(),
        P("expert", None, "dp", None),
        P("expert", None, "dp", None),
        P("expert", None, "dp", None),
        P("expert", None, "dp", None),
        P("expert", None, "dp"),
    )
    out_specs = (P("expert", None, "dp"), P("expert", None, "dp", None), P("expert", None, "dp"))
    return jax.shard_map(body, mesh=mesh, in_specs=in_specs, out_specs=out_specs, check_vma=False)
```

```python
import itertools

import jax
import jax.numpy as jnp
import numpy as np
from jax import lax
from jax.sharding import PartitionSpec as P

learning_rate = 0.01
beta_first = 0.9
beta_second = 0.999
adam_epsilon = 1e-08
bias_first = 1.0 - 0.9**10
bias_second = 1.0 - 0.999**10


def adam_update(weights, grads, first_moment, second_moment):
    grad_float = grads.astype(jnp.float32)
    first_new = beta_first * first_moment + (1.0 - beta_first) * grad_float
    second_new = beta_second * second_moment + (1.0 - beta_second) * grad_float * grad_float
    adam_step = first_new / bias_first / (jnp.sqrt(second_new / bias_second) + adam_epsilon)
    return (weights.astype(jnp.float32) - learning_rate * adam_step).astype(jnp.bfloat16)


max_levels = 4


def partial_products(slots, pieces):
    total, start = 0.0, 0
    for updated in pieces:
        rows = updated.shape[1]
        joined = jnp.concatenate([updated[0], updated[1]], axis=1)
        total += jnp.dot(
            slots[:, start : start + rows], joined, preferred_element_type=jnp.float32
        )
        start += rows
    return total.astype(jnp.bfloat16)


def dp_blocks(partials):
    parts = lax.axis_size("dp")
    return lax.all_to_all(
        partials.reshape(1, parts, -1, partials.shape[1]),
        "dp",
        split_axis=1,
        concat_axis=1,
        tiled=True,
    )


def finish_rows(blocks, down_local):
    width = down_local.shape[0]
    summed = jnp.sum(blocks[0].astype(jnp.float32), axis=0)
    hidden = (jax.nn.silu(summed[:, :width]) * summed[:, width:]).astype(jnp.bfloat16)
    result = jnp.dot(
        lax.all_gather(hidden, "dp", axis=0, tiled=True),
        down_local,
        preferred_element_type=jnp.float32,
    )
    return result.astype(jnp.bfloat16)


def owner_exchange(pieces):
    return lax.all_to_all(pieces, "expert", split_axis=1, concat_axis=1, tiled=True)


def two_phase_migration(plan, updated, down_local):
    owners = lax.axis_size("expert")
    local_rows, width = updated.shape[1:]
    expert_ids = jnp.arange(owners, dtype=jnp.int32)
    spread_down = owner_exchange(down_local.reshape(1, owners, width // owners, local_rows))
    spread_proj = owner_exchange(updated.reshape(2, owners, local_rows // owners, width))
    inverse = jnp.sum(
        jnp.where(plan[None, :] == expert_ids[:, None], expert_ids[None, :], 0), axis=1
    )
    moved_down = owner_exchange(jnp.take(spread_down, inverse, axis=1))
    moved_proj = owner_exchange(jnp.take(spread_proj, inverse, axis=1))
    return moved_proj.reshape(2, local_rows, width), moved_down.reshape(width, local_rows)


def colour_table(levels):
    bits = np.array(list(itertools.product((0, 1), repeat=levels)), np.int32)
    return np.stack([bits, 1 - bits], axis=2).reshape(len(bits), 2 * levels)


def worst_cut(perm):
    worst = 0
    for cut in range(1, len(perm)):
        up = sum(1 for z, to in enumerate(perm) if z < cut <= to)
        worst = max(worst, up)
    return worst


def route_choice(plan, levels):
    owners = 2 * levels
    perms = list(itertools.permutations(range(levels)))
    colours = colour_table(levels)
    ids = jnp.arange(owners, dtype=jnp.int32)
    arrives = plan[:, None] == ids[None, :]
    landed = jnp.sum(jnp.where(arrives[None], colours[:, :, None], 0), axis=1)
    pair_sum = landed.reshape(-1, levels, 2).sum(axis=2)
    bad = jnp.sum((pair_sum != 1).astype(jnp.int32), axis=1)
    scale = np.repeat(levels ** np.arange(levels, dtype=np.int32), 2)
    term = (plan // 2) * scale
    codes = np.array([sum(to * levels**z for z, to in enumerate(p)) for p in perms], np.int32)
    costs = np.array([worst_cut(p) for p in perms], np.int32)
    keys = [
        jnp.sum(jnp.where(colours == colour, term[None, :], 0), axis=1) for colour in (0, 1)
    ]
    hits = [key[:, None] == codes[None, :] for key in keys]
    cost = sum(jnp.sum(jnp.where(hit, costs[None, :], 0), axis=1) for hit in hits)
    count = len(colours)
    order = (bad * (4 * levels) + cost) * count + jnp.arange(count, dtype=jnp.int32)
    chosen = jnp.arange(count, dtype=jnp.int32) == jnp.min(order) % count
    numbers = np.arange(len(perms), dtype=np.int32)
    picks = [
        jnp.sum(jnp.where(chosen[:, None] & hit, numbers[None, :], 0)) for hit in hits
    ]
    source = jnp.sum(jnp.where(chosen[:, None], colours, 0), axis=0)
    landing = jnp.sum(jnp.where(chosen[:, None], landed, 0), axis=0)
    return source, landing, picks, perms


def body(
    tokens, routes, gates, plan, proj_weight, proj_grad, first_moment, second_moment, down_weight
):
    owners = lax.axis_size("expert")
    local_rows = proj_weight.shape[2]
    width = proj_weight.shape[3]
    levels = owners // 2
    routable = levels <= max_levels and foldable(local_rows, width)

    def updated_rows(grads, a, b):
        return adam_update(
            proj_weight[0, :, a:b], grads[0, :, a:b], first_moment[0, :, a:b], second_moment[0, :, a:b]
        )

    group_tokens = tokens.shape[1]
    route_count = routes.shape[2]
    capacity = min(group_tokens, 3 * group_tokens * route_count // (2 * owners))
    down_local = down_weight[0]
    expert_ids = jnp.arange(owners, dtype=jnp.int32)
    target_match = routes[0][:, :, None] == expert_ids[None, None, :]
    routed = jnp.sum(target_match.astype(jnp.int32), axis=1)
    weighting = jnp.sum(jnp.where(target_match, gates[0][:, :, None], 0.0), axis=1)
    ranks = jnp.cumsum(routed, axis=0) - routed
    slot_ids = jnp.arange(capacity, dtype=jnp.int32)
    select = jnp.logical_and(
        ranks.T[:, None, :] == slot_ids[None, :, None], routed.T[:, None, :] > 0
    )
    dispatch_buf = jnp.einsum(
        "ost,td->osd", select.astype(jnp.bfloat16), tokens[0], preferred_element_type=jnp.float32
    ).astype(jnp.bfloat16)
    arrived = owner_exchange(dispatch_buf[None])
    slots = arrived.reshape(owners * capacity, local_rows)


    def experts(pieces):
        expert_out = finish_rows(dp_blocks(partial_products(slots, pieces)), down_local)
        return expert_out.reshape(1, owners, capacity, local_rows)

    if routable:
        early = early_rows(local_rows, width)
        new_proj, new_down, returned = routed_migration(
            plan,
            levels,
            updated_rows(proj_grad, 0, early),
            lambda grads: updated_rows(grads, early, local_rows),
            proj_grad,
            down_local,
            arrived,
            experts,
        )
    else:
        updated = updated_rows(proj_grad, 0, local_rows)
        new_proj, new_down = two_phase_migration(plan, updated, down_local)
        returned = owner_exchange(experts([updated]))
    combine = select.astype(jnp.float32) * weighting.T[:, None, :]
    mixed = jnp.einsum(
        "ost,osd->td", combine, returned[0].astype(jnp.float32), precision=lax.Precision.HIGHEST
    )
    return (mixed.astype(jnp.bfloat16)[None], new_proj[None], new_down[None])


def foldable(local_rows, width):
    extra = local_rows - width
    return extra > 0 and width % extra == 0 and (width // 2) % (width // extra) == 0


def early_rows(local_rows, width):
    return (local_rows - (width // 2) * local_rows // width) // 2


def fold(half, width):
    strips = width // (half.shape[1] - width)
    tall = half.shape[0] // strips
    rest = [half[i * tall : (i + 1) * tall, width:] for i in range(strips)]
    return [half[:, :width], jnp.concatenate(rest, axis=1)]


def unfold(packed, rows, columns):
    width = packed.shape[1]
    extra = columns - width
    strips = [packed[rows:, i * extra : (i + 1) * extra] for i in range(width // extra)]
    return jnp.concatenate([packed[:rows], jnp.concatenate(strips, axis=0)], axis=1)


def routed_migration(
    plan, levels, updated_early, late_rows, grads, down_local, arrived, experts
):
    source, landing, picks, perms = route_choice(plan, levels)
    me = lax.axis_index("expert")
    line = me % 2
    at_me = jnp.arange(2 * levels, dtype=jnp.int32) == me
    colour = jnp.sum(jnp.where(at_me, source, 0))
    landing_colour = jnp.sum(jnp.where(at_me, landing, 0))
    kept_half = line ^ colour
    final_half = line ^ landing_colour
    across = [(e, e ^ 1) for e in range(2 * levels)]
    local_rows, width = down_local.shape[1], updated_early.shape[2]
    half_width = width // 2
    folded = half_width * local_rows // width

    def swap(value):
        return lax.ppermute(value, "expert", across)

    def parted(first, second):
        keep = jnp.where(kept_half == 0, first, second)
        send = jnp.where(kept_half == 0, second, first)
        return keep, send

    def coloured(keep, other):
        first = jnp.where(colour == 0, keep, other)
        second = jnp.where(colour == 0, other, keep)
        return first, second

    packed = [
        jnp.concatenate(
            fold(down_local[h * half_width : (h + 1) * half_width], width)
            + [updated_early[h]],
            axis=0,
        )
        for h in (0, 1)
    ]
    keep_p, send_p = parted(*packed)
    send_p, grads, ahead = lax.optimization_barrier((send_p, grads, arrived))
    crossed_p = swap(send_p)
    updated_late = late_rows(grads)
    keep_q, send_q = parted(updated_late[0], updated_late[1])
    expert_out = experts([updated_early, updated_late])
    keep_p, crossed_p, keep_q, send_q, expert_out = lax.optimization_barrier(
        (keep_p, crossed_p, keep_q, send_q, expert_out)
    )

    def along(perm):
        pairs = [(2 * z + x, 2 * to + x) for z, to in enumerate(perm) for x in (0, 1)]
        return lambda value: lax.ppermute(value, "expert", pairs)

    def first_stage(perm):
        move = along(perm)
        return lambda value, crossing: (move(value), swap(crossing))

    def step(number, carry):
        keep, crossed, moved, arrived, unused = carry
        first, second = coloured(keep, crossed)
        own = jnp.where(landing_colour == 0, moved, arrived)
        other = jnp.where(landing_colour == 0, arrived, moved)
        crossing = jnp.where(number == 0, moved, other)
        moved, crossed = lax.switch(
            picks[0], [first_stage(p) for p in perms], first, crossing
        )
        arrived = lax.switch(picks[1], [along(p) for p in perms], second)
        return keep_q, crossed, moved, arrived, own

    blank = jnp.zeros_like(send_q)
    unused, other_p, moved, arrived, own_p = lax.fori_loop(
        0, 2, step, (keep_p, crossed_p, send_q, blank, blank)
    )
    moved, arrived, expert_out = lax.optimization_barrier((moved, arrived, expert_out))
    returned = owner_exchange(expert_out)
    own_q = jnp.where(landing_colour == 0, moved, arrived)
    send_q = jnp.where(landing_colour == 0, arrived, moved)
    send_q, returned = lax.optimization_barrier((send_q, returned))
    other_q = swap(send_q)
    halves_p = [jnp.where(final_half == h, own_p, other_p) for h in (0, 1)]
    halves_q = [jnp.where(final_half == h, own_q, other_q) for h in (0, 1)]
    new_down = jnp.concatenate(
        [unfold(half[:folded], half_width, local_rows) for half in halves_p], axis=0
    )
    new_proj = jnp.stack(
        [jnp.concatenate([p[folded:], q], axis=0) for p, q in zip(halves_p, halves_q)]
    )
    return new_proj, new_down, returned


def solution(mesh):
    in_specs = (
        P("expert", None, "dp"),
        P("expert", None, None),
        P("expert", None, None),
        P(),
        P("expert", None, "dp", None),
        P("expert", None, "dp", None),
        P("expert", None, "dp", None),
        P("expert", None, "dp", None),
        P("expert", None, "dp"),
    )
    out_specs = (P("expert", None, "dp"), P("expert", None, "dp", None), P("expert", None, "dp"))
    return jax.shard_map(body, mesh=mesh, in_specs=in_specs, out_specs=out_specs, check_vma=False)
```
